32 devices in a mesh: seq: 16 (over z, y, x), mp: 2 (over core).
Axes of the slice: x: 2, y: 2, z: 4, core: 2. Of those that a mesh axis runs over, the one named last changes fastest.
Arguments:
- layer_input: bfloat16 [128, 8192], P('seq'), may hold values from -6 to 6
- w_query: bfloat16 [8192, 8192], P('seq', 'mp'), may hold values from -0.0625 to 0.0625
- w_key: bfloat16 [8192, 1024], P('seq', 'mp'), may hold values from -0.1875 to 0.1875
- w_value: bfloat16 [8192, 1024], P('seq', 'mp'), may hold values from -0.0625 to 0.0625
- w_out: bfloat16 [8192, 8192], P('mp', 'seq'), may hold values from -0.0625 to 0.0625
- kv_cache: bfloat16 [2, 32, 4096, 1024], P(None, None, 'seq', 'mp'), may hold values from -180 to 180, as said below
- cache_len: int32 [32], replicated, may hold values from 1 to 4096, as said below
Outputs:
- attn_out: bfloat16 [128, 8192], P('mp', 'seq')
The draws below stay inside these ranges and needn't reach their ends.
Inputs may be any that keep to these rules, and one draw needn't show every extreme that they name: kv_cache entries at positions at or beyond a request's cache_len are never read. `cache_len`: exactly 4096 for at least one request.
All inputs are finite; a program needn't handle non-finite values.
Results may differ from the reference program's by a relative error of at most 0.012.
The reference program's roundings to bfloat16 on the way (of `normed`, `queries`, `values_new` and `attended`) count: a program that leaves them out, or rounds other values in their place, can miss the bound.
Values may be sent and summed in bfloat16 or wider, within the bound.
A program may use at most 192 MiB of HBM per device.

```python
import math
import jax
import jax.numpy as jnp
from jax import lax

D = 8192
HQ = 64
KVH = 8
HD = 128
REQUEST_TOTAL = 32
STEPS = 4
ROWS = 128
CONTEXT_SLOTS = 4096


def draw_kv_cache(key, part):
    key_a, key_b = jax.random.split(key, 2)
    cache_shape = (REQUEST_TOTAL, CONTEXT_SLOTS, KVH * HD)
    key_portion = jnp.clip(2.5 * jax.random.normal(key_a, cache_shape, jnp.float32), -15.0, 15.0)
    value_part = jnp.clip(jax.random.normal(key_b, cache_shape, jnp.float32), -6.0, 6.0)
    return jnp.stack([key_portion, value_part]).astype(jnp.bfloat16)


def draw_cache_len(key, part):
    key_a, key_b = jax.random.split(key, 2)
    drawn = jax.random.randint(key_a, (REQUEST_TOTAL,), 1, CONTEXT_SLOTS + 1, dtype=jnp.int32)
    longest = jax.random.randint(key_b, (), 0, REQUEST_TOTAL, dtype=jnp.int32)
    return jnp.where(jnp.arange(REQUEST_TOTAL, dtype=jnp.int32) == longest, CONTEXT_SLOTS, drawn).astype(jnp.int32)


def levels(rng, shape, pieces, least, high):
    def one(axis_at, parts):
        draws = jax.random.uniform(jax.random.fold_in(jax.random.fold_in(rng, 6), axis_at), (parts,), jnp.float32, least / len(pieces), high / len(pieces))
        return jnp.repeat(jnp.exp(draws), shape[axis_at] // parts).reshape((-1,) + (1,) * (len(shape) - axis_at - 1))

    level = one(*pieces[0])
    for cut in pieces[1:]:
        level = level * one(*cut)
    return level


def normal_values(rng, extent, width, reach, pieces=(), held_as=jnp.bfloat16):
    loudness = levels(rng, extent, pieces, -0.22, 0.18) if pieces else 1.0
    entries = jax.random.normal(rng, extent, jnp.float32) * width * loudness
    return jnp.minimum(jnp.maximum(entries, -reach), reach).astype(held_as)


def setup_inputs(seed: int = 0) -> dict:
    arg_keys = jax.random.split(jax.random.key(seed), 8)
    layer_input = normal_values(arg_keys[0], (ROWS, D), 1.0, 6.0, ((0, 16),))
    w_query = normal_values(arg_keys[1], (D, HQ * HD), D ** -0.5, 0.0625, ((0, 16), (1, 2)))
    w_key = normal_values(arg_keys[2], (D, KVH * HD), (D // 9) ** -0.5, 0.1875, ((0, 16), (1, 2)))
    w_value = normal_values(arg_keys[3], (D, KVH * HD), D ** -0.5, 0.0625, ((0, 16), (1, 2)))
    w_out = normal_values(arg_keys[4], (HQ * HD, D), (HQ * HD) ** -0.5, 0.0625, ((0, 2), (1, 16)))
    kv_cache = draw_kv_cache(jax.random.fold_in(arg_keys[7], 71), 0)
    cache_len = draw_cache_len(jax.random.fold_in(arg_keys[7], 71), 0)
    return dict(layer_input=layer_input, w_query=w_query, w_key=w_key, w_value=w_value, w_out=w_out, kv_cache=kv_cache, cache_len=cache_len)


NEG_FILL = -1e+30

def inverse_freq():
    index = jnp.arange(HD // 2, dtype=jnp.float32)
    base_freq = jnp.exp(-(2.0 * index / HD) * math.log(500000.0))
    wavelength = 2.0 * math.pi / base_freq
    smooth = jnp.clip((8192.0 / wavelength - 1.0) / 3.0, 0.0, 1.0)
    return (1.0 - smooth) * base_freq / 8.0 + smooth * base_freq

def rotate(values, positions):
    angles = positions.astype(jnp.float32)[..., None] * inverse_freq()
    cosine = jnp.cos(angles)
    sines = jnp.sin(angles)
    half_width = HD // 2
    first_half = values[..., :half_width]
    second_half = values[..., half_width:]
    return jnp.concatenate([first_half * cosine - second_half * sines, second_half * cosine + first_half * sines], axis=-1)

def reference(layer_input, w_query, w_key, w_value, w_out, kv_cache, cache_len):
    widened = layer_input.astype(jnp.float32)
    normed = (widened * lax.rsqrt(lax.optimization_barrier(jnp.mean(widened * widened, axis=-1, keepdims=True)) + 1e-05)).astype(jnp.bfloat16)
    query_all = jnp.dot(normed, w_query, preferred_element_type=jnp.float32)
    key_all = jnp.dot(normed, w_key, preferred_element_type=jnp.float32)
    value_all = jnp.dot(normed, w_value, preferred_element_type=jnp.float32)
    positions = (cache_len[:, None] + jnp.arange(STEPS, dtype=jnp.int32)[None, :]).reshape(ROWS)
    queries = rotate(query_all.reshape(ROWS, HQ, HD), positions[:, None]).astype(jnp.bfloat16)
    keys_new = rotate(key_all.reshape(ROWS, KVH, HD), positions[:, None]).astype(jnp.bfloat16)
    values_new = value_all.astype(jnp.bfloat16).reshape(ROWS, KVH, HD)
    group_size = HQ // KVH
    score_scale = 1.0 / math.sqrt(HD)
    causal = jnp.arange(STEPS)[:, None] >= jnp.arange(STEPS)[None, :]
    highest = lax.Precision.HIGHEST

    def one_request(request):
        first_row = (request * STEPS).astype(jnp.int32)
        query_rows = lax.dynamic_slice_in_dim(queries, first_row, STEPS, 0).reshape(STEPS, KVH, group_size, HD).astype(jnp.float32)
        key_rows = lax.dynamic_slice_in_dim(keys_new, first_row, STEPS, 0).astype(jnp.float32)
        value_rows = lax.dynamic_slice_in_dim(values_new, first_row, STEPS, 0).astype(jnp.float32)
        cache_keys = kv_cache[0, request].reshape(CONTEXT_SLOTS, KVH, HD).astype(jnp.float32)
        cache_values = kv_cache[1, request].reshape(CONTEXT_SLOTS, KVH, HD).astype(jnp.float32)
        active_slot = jnp.arange(CONTEXT_SLOTS, dtype=jnp.int32) < cache_len[request]
        old_scores = jnp.einsum('tkgd,pkd->kgtp', query_rows, cache_keys, precision=highest) * score_scale
        old_scores = jnp.where(active_slot, old_scores, NEG_FILL)
        new_scores = jnp.einsum('tkgd,ukd->kgtu', query_rows, key_rows, precision=highest) * score_scale
        new_scores = jnp.where(causal, new_scores, NEG_FILL)
        row_top = jnp.maximum(lax.optimization_barrier(jnp.max(old_scores, axis=-1)), lax.optimization_barrier(jnp.max(new_scores, axis=-1)))
        old_weights = jnp.where(active_slot, jnp.exp(old_scores - row_top[..., None]), 0.0)
        new_weights = jnp.where(causal, jnp.exp(new_scores - row_top[..., None]), 0.0)
        denominator = lax.optimization_barrier(jnp.sum(old_weights, axis=-1)) + lax.optimization_barrier(jnp.sum(new_weights, axis=-1))
        pooled = jnp.einsum('kgtp,pkd->kgtd', old_weights, cache_values, precision=highest)
        pooled = pooled + jnp.einsum('kgtu,ukd->kgtd', new_weights, value_rows, precision=highest)
        attended = pooled / denominator[..., None]
        return attended.transpose(2, 0, 1, 3).reshape(STEPS, HQ * HD).astype(jnp.bfloat16)
    attended = lax.map(one_request, jnp.arange(REQUEST_TOTAL, dtype=jnp.int32)).reshape(ROWS, HQ * HD)
    return jnp.dot(attended, w_out, preferred_element_type=jnp.float32).astype(jnp.bfloat16)
```

```python
import functools
import math

import jax
import jax.numpy as jnp
from jax import lax
from jax.experimental import pallas as pl
from jax.experimental.pallas import tpu as pltpu
from jax.sharding import PartitionSpec as P

HD = 128


NEG_FILL = -1e30


def inverse_freq():
    index = jnp.arange(HD // 2, dtype=jnp.float32)
    base_freq = jnp.exp(-(2.0 * index / HD) * math.log(500000.0))
    wavelength = 2.0 * math.pi / base_freq
    smooth = jnp.clip((8192.0 / wavelength - 1.0) / 3.0, 0.0, 1.0)
    return (1.0 - smooth) * base_freq / 8.0 + smooth * base_freq


def rotate(values, positions):
    angles = positions.astype(jnp.float32)[..., None] * inverse_freq()
    cosine = jnp.cos(angles)
    sines = jnp.sin(angles)
    half_width = HD // 2
    first_half = values[..., :half_width]
    second_half = values[..., half_width:]
    return jnp.concatenate(
        [first_half * cosine - second_half * sines, second_half * cosine + first_half * sines],
        axis=-1,
    )


def shards(layer_input, w_query, w_key, w_value, w_out, kv_cache, cache_len):
    widened = layer_input.astype(jnp.float32)
    normed = (
        widened * lax.rsqrt(jnp.mean(widened * widened, axis=-1, keepdims=True) + 1e-05)
    ).astype(jnp.bfloat16)
    gathered = lax.all_to_all(normed, "seq", split_axis=1, concat_axis=0, tiled=True)
    partial_query = jnp.dot(gathered, w_query, preferred_element_type=jnp.float32)
    partial_key = jnp.dot(gathered, w_key, preferred_element_type=jnp.float32)
    partial_value = jnp.dot(gathered, w_value, preferred_element_type=jnp.float32)
    row_count = gathered.shape[0]
    request_count = cache_len.shape[0]
    decode_count = row_count // request_count
    heads_here = partial_query.shape[1] // HD
    kv_here = partial_key.shape[1] // HD
    group_size = heads_here // kv_here
    score_scale = 1.0 / math.sqrt(HD)
    highest = lax.Precision.HIGHEST
    query_all, key_all, value_all = lax.psum((partial_query, partial_key, partial_value), "seq")
    positions = (cache_len[:, None] + jnp.arange(decode_count, dtype=jnp.int32)[None, :]).reshape(
        row_count
    )
    queries = rotate(query_all.reshape(row_count, heads_here, HD), positions[:, None]).astype(
        jnp.bfloat16
    )
    keys_new = rotate(key_all.reshape(row_count, kv_here, HD), positions[:, None]).astype(
        jnp.bfloat16
    )
    values_new = value_all.astype(jnp.bfloat16)
    queries = queries.reshape(request_count, decode_count, kv_here, group_size, HD)
    keys_new = keys_new.reshape(request_count, decode_count, kv_here, HD)
    values_new = values_new.reshape(request_count, decode_count, kv_here, HD)
    block_size = kv_cache.shape[2]
    cache_keys = kv_cache[0].reshape(request_count, block_size, kv_here, HD)
    cache_values = kv_cache[1].reshape(request_count, block_size, kv_here, HD).astype(jnp.float32)
    first_slot = lax.axis_index("seq") * block_size
    slot_index = first_slot + jnp.arange(block_size, dtype=jnp.int32)
    active_slot = (slot_index[None, :] < cache_len[:, None])[:, None, None, None, :]
    causal = (jnp.arange(decode_count)[:, None] >= jnp.arange(decode_count)[None, :])[
        None, None, None
    ]
    old_scores = (
        jnp.einsum("rtkgd,rpkd->rkgtp", queries, cache_keys, preferred_element_type=jnp.float32)
        * score_scale
    )
    old_scores = jnp.where(active_slot, old_scores, NEG_FILL)
    old_top = jnp.max(old_scores, axis=-1)
    new_scores = (
        jnp.einsum("rtkgd,rukd->rkgtu", queries, keys_new, preferred_element_type=jnp.float32)
        * score_scale
    )
    new_scores = jnp.where(causal, new_scores, NEG_FILL)
    new_top = jnp.max(new_scores, axis=-1)
    row_top = lax.pmax(jnp.maximum(old_top, new_top), "seq")
    old_weights = jnp.where(active_slot, jnp.exp(old_scores - row_top[..., None]), 0.0)
    old_total, old_pooled = lax.psum(
        (
            jnp.sum(old_weights, axis=-1),
            jnp.einsum("rkgtp,rpkd->rkgtd", old_weights, cache_values, precision=highest),
        ),
        "seq",
    )
    new_weights = jnp.where(causal, jnp.exp(new_scores - row_top[..., None]), 0.0)
    denominator = old_total + jnp.sum(new_weights, axis=-1)
    pooled = old_pooled + jnp.einsum(
        "rkgtu,rukd->rkgtd", new_weights, values_new.astype(jnp.float32), precision=highest
    )
    attended = (
        (pooled / denominator[..., None])
        .transpose(0, 3, 1, 2, 4)
        .reshape(row_count, heads_here * HD)
        .astype(jnp.bfloat16)
    )
    return lax.psum_scatter(
        jnp.dot(attended, w_out, preferred_element_type=jnp.float32).astype(jnp.bfloat16),
        "mp",
        scatter_dimension=0,
        tiled=True,
    )


def fused_kernel(
    n, steps, scale, cos_ref, sin_ref, len_ref, x_ref, wq_hbm, wk_hbm, wv_hbm, wo_hbm, kv_hbm,
    out_ref,
    wq, wk, wv, wo, kv, nsend, xrecv, psend, prec, zsend, zrecv, acc, qall, knew, vnew,
    osend, lsend, orecv, lrecv, accf, attg, pf, msend, mrecv,
    w_sem, kv_sem, s_x, r_x, s_o, r_o, s_l, r_l, s_q, r_q, s_a, r_a, s_p, r_p, s_z, r_z, m_sem,
):
    me = lax.axis_index("seq")
    core = lax.axis_index("mp")
    f32, bf16 = jnp.float32, jnp.bfloat16
    rp, width = x_ref.shape
    depth = width // n
    rows = n * rp
    heads = wq.shape[1] // HD
    kvh = wk.shape[1] // HD
    group = heads // kvh
    per = rp // steps
    block = kv.shape[2]
    qcols = heads * HD
    kcols = kvh * HD

    weights = [
        pltpu.make_async_copy(wq_hbm, wq, w_sem.at[0]),
        pltpu.make_async_copy(wk_hbm, wk, w_sem.at[1]),
        pltpu.make_async_copy(wv_hbm, wv, w_sem.at[2]),
    ]
    out_weight = pltpu.make_async_copy(wo_hbm, wo, w_sem.at[3])

    def cache_copy(j):
        at = (slice(None), pl.ds(j * per, per))
        return pltpu.make_async_copy(kv_hbm.at[at], kv.at[at], kv_sem.at[j])

    for copy in weights:
        copy.start()

    barrier = pltpu.get_barrier_semaphore()

    def greet(d, _):
        pl.semaphore_signal(barrier, inc=1, device_id={"seq": lax.rem(me + d, n)},
                            device_id_type=pl.DeviceIdType.MESH)
        return _

    lax.fori_loop(1, n, greet, 0)
    pl.semaphore_signal(barrier, inc=1, device_id={"mp": 1 - core},
                        device_id_type=pl.DeviceIdType.MESH)

    def remote(src, dst, send, recv, d):
        return pltpu.make_async_remote_copy(
            src_ref=src, dst_ref=dst, send_sem=send.at[d], recv_sem=recv.at[d],
            device_id={"seq": lax.rem(me + d, n)}, device_id_type=pl.DeviceIdType.MESH)

    def x_copy(d):
        return remote(nsend.at[lax.rem(me + d, n)], xrecv.at[me], s_x, r_x, d)

    def o_copy(j, slot):
        return pltpu.make_async_remote_copy(
            src_ref=osend.at[j], dst_ref=orecv.at[slot], send_sem=s_o.at[j], recv_sem=r_o.at[slot],
            device_id={"seq": j}, device_id_type=pl.DeviceIdType.MESH)

    def l_copy(j, slot):
        return pltpu.make_async_remote_copy(
            src_ref=lsend.at[j], dst_ref=lrecv.at[slot], send_sem=s_l.at[j], recv_sem=r_l.at[slot],
            device_id={"seq": j}, device_id_type=pl.DeviceIdType.MESH)

    deep = n // 4
    x_at, y_at, z_at = lax.rem(me, 2), lax.rem(lax.div(me, 2), 2), lax.div(me, 4)
    x_peer = me + 1 - 2 * x_at
    y_peer = me + 2 - 4 * y_at

    def source(kind, dz):
        z = lax.rem(z_at - dz + deep, deep)
        x = x_at + lax.rem(kind, 2) * (1 - 2 * x_at)
        y = y_at + lax.div(kind, 2) * (1 - 2 * y_at)
        return z * 4 + y * 2 + x

    def p_copy(dz, kind):
        return pltpu.make_async_remote_copy(
            src_ref=psend.at[source(kind, deep - dz)], dst_ref=prec.at[dz, kind - 1],
            send_sem=s_p.at[dz, kind], recv_sem=r_p.at[dz, kind],
            device_id={"seq": source(kind, 0)}, device_id_type=pl.DeviceIdType.MESH)

    def z_copy(dz):
        return remote(zsend.at[dz], zrecv.at[dz], s_z, r_z, 4 * dz)

    class Gather:
        def __init__(self, ref, low, high, send, recv):
            self.ref, self.low, self.high, self.send, self.recv = ref, low, high, send, recv

        def copy(self, view, way, dz, target):
            return pltpu.make_async_remote_copy(
                src_ref=view, dst_ref=view, send_sem=self.send.at[way, dz],
                recv_sem=self.recv.at[way, dz],
                device_id={"seq": target}, device_id_type=pl.DeviceIdType.MESH)

        def z(self, dz):
            return self.copy(self.ref.at[me], 0, dz, lax.rem(me + 4 * dz, n))

        def x(self, dz):
            return self.copy(self.ref.at[source(0, dz)], 1, dz, x_peer)

        def y(self, dz):
            return self.copy(self.ref.at[source(0, dz)], 2, dz, y_peer)

        def xy(self, dz):
            return self.copy(self.low(self.ref, source(1, dz)), 3, dz, y_peer)

        def yx(self, dz):
            return self.copy(self.high(self.ref, source(2, dz)), 4, dz, x_peer)

        def begin(self):
            each(lambda dz: self.z(dz).start(), 1, deep)
            self.x(0).start()
            self.y(0).start()

        def spread(self, dz):
            self.z(dz).wait_recv()
            self.x(dz).start()
            self.y(dz).start()

        def forward(self, dz):
            self.x(dz).wait_recv()
            self.xy(dz).start()
            self.y(dz).wait_recv()
            self.yx(dz).start()

        def finish(self, dz):
            self.xy(dz).wait_recv()
            self.yx(dz).wait_recv()

        def sent(self, dz):
            self.x(dz).wait_send()
            self.y(dz).wait_send()
            self.xy(dz).wait_send()
            self.yx(dz).wait_send()

        def drain(self):
            each(lambda dz: self.z(dz).wait_send(), 1, deep)
            each(self.sent, 0, deep)

    def each(action, first=1, last=n):
        def body(d, _):
            action(d)
            return _
        lax.fori_loop(first, last, body, 0)

    some = heads // 2
    queries = Gather(qall, lambda ref, j: ref.at[j, 0:some], lambda ref, j: ref.at[j, some:heads],
                     s_q, r_q)
    results = Gather(attg, lambda ref, j: ref.at[j, :, 0:some * HD],
                     lambda ref, j: ref.at[j, :, some * HD:qcols], s_a, r_a)

    widened = x_ref[...].astype(f32)
    norm = widened * lax.rsqrt(jnp.mean(widened * widened, axis=-1, keepdims=True) + 1e-05)
    for j in range(n):
        nsend[j] = norm[:, j * depth:(j + 1) * depth].astype(bf16)
    xrecv[me] = nsend[me]
    pl.semaphore_wait(barrier, n)
    each(lambda d: x_copy(d).start())
    each(lambda d: cache_copy(d).start(), 0)
    out_weight.start()
    for copy in weights:
        copy.wait()
    each(lambda d: x_copy(d).wait_recv())

    gathered = xrecv[...].astype(f32).reshape(rows, depth).astype(bf16)

    def project(weight, count, first):
        tile = min(512, count)
        for c in range(count // tile):
            part = jnp.dot(gathered, weight[:, c * tile:(c + 1) * tile], preferred_element_type=f32)
            psend[:, :, first + c * tile:first + (c + 1) * tile] = part.reshape(
                n, rp, tile).astype(bf16)

    project(wq, qcols, 0)
    project(wk, kcols, qcols)
    project(wv, kcols, qcols + kcols)

    def release(dz):
        for kind in (3, 1, 2):
            p_copy(dz, kind).start()

    def plane_sum(dz):
        total = psend[source(0, deep - dz)].astype(f32)
        for kind in (3, 1, 2):
            p_copy(dz, kind).wait_recv()
        for kind in (3, 1, 2):
            total += prec[dz, kind - 1].astype(f32)
        return total

    def pass_on(dz):
        zsend[dz] = plane_sum(dz)
        z_copy(dz).start()

    def add(dz):
        z_copy(dz).wait_recv()
        acc[...] += zrecv[dz]

    each(release, 1, deep)
    release(0)
    each(pass_on, 1, deep)
    acc[...] = plane_sum(0)
    each(add, 1, deep)

    cosine = cos_ref[...]
    sines = sin_ref[...]

    def turn(column):
        value = acc[:, column:column + HD]
        return value * cosine + pltpu.roll(value, HD // 2, 1) * sines

    for h in range(heads):
        qall[me, h] = turn(h * HD).astype(bf16)
    queries.begin()
    for k in range(kvh):
        knew[k] = jnp.zeros(knew.shape[1:], bf16)
        vnew[k] = jnp.zeros(vnew.shape[1:], bf16)
        knew[k, 0:rp] = turn(qcols + k * HD).astype(bf16)
        column = qcols + kcols + k * HD
        vnew[k, 0:rp] = acc[:, column:column + HD].astype(bf16)

    lane = lax.broadcasted_iota(jnp.int32, (rp, HD), 1)
    m_rows = group * rp

    def attend(query, keys, values, bias, o_ref, l_ref, at):
        stats = jnp.zeros((rp, HD), f32)
        for k in range(kvh):
            q = query(k).astype(f32).reshape(m_rows, HD).astype(bf16)
            scores = lax.dot_general(q, keys(k), (((1,), (1,)), ((), ())),
                                     preferred_element_type=f32) * scale + bias
            top = jnp.max(scores, axis=-1, keepdims=True)
            weight = jnp.exp(scores - top)
            total = jnp.sum(weight, axis=-1, keepdims=True)
            pooled = jnp.dot(weight.astype(bf16), values(k), preferred_element_type=f32)
            pooled = pooled * (1.0 / total)
            o_ref[at, k * group:(k + 1) * group] = pooled.reshape(group, rp, HD).astype(bf16)
            level = top + jnp.log(total)
            for g in range(group):
                stats = jnp.where(lane == k * group + g, level[g * rp:(g + 1) * rp], stats)
        l_ref[at] = stats

    new = knew.shape[1]
    row = lax.rem(lax.broadcasted_iota(jnp.int32, (m_rows, new), 0), rp)
    col = lax.broadcasted_iota(jnp.int32, (m_rows, new), 1)
    seen = (col <= row) & (lax.div(col, steps) == lax.div(row, steps))
    attend(lambda k: qall[me, k * group:(k + 1) * group], lambda k: knew[k], lambda k: vnew[k],
           jnp.where(seen, 0.0, NEG_FILL), orecv, lrecv, n)

    span = per * block
    row_request = lax.div(lax.rem(lax.broadcasted_iota(jnp.int32, (m_rows, span), 0), rp), steps)
    slot = lax.broadcasted_iota(jnp.int32, (m_rows, span), 1)

    def cached(j, o_ref, l_ref):
        cache_copy(j).wait()
        bias = jnp.full((m_rows, span), NEG_FILL, f32)
        for r in range(per):
            left = len_ref[j * per + r] - me * block
            live = (row_request == r) & (slot >= r * block) & (slot < r * block + jnp.minimum(left, block))
            bias = jnp.where(live, 0.0, bias)
        here = pl.ds(j * per, per)
        attend(lambda k: qall[j, k * group:(k + 1) * group],
               lambda k: kv[0, here, :, k * HD:(k + 1) * HD].reshape(span, HD),
               lambda k: kv[1, here, :, k * HD:(k + 1) * HD].reshape(span, HD),
               bias, o_ref, l_ref, j)

    def answer(j):
        cached(j, osend, lsend)
        o_copy(j, me).start()
        l_copy(j, me).start()

    queries.forward(0)
    cached(me, orecv, lrecv)
    each(queries.spread, 1, deep)

    def own_line(dz):
        answer(source(0, dz))
        queries.forward(dz)

    each(own_line, 1, deep)
    each(lambda i: answer(source(1 + lax.div(i, deep), lax.rem(i, deep))), 0, 2 * deep)

    def diagonal(dz):
        queries.finish(dz)
        answer(source(3, dz))

    each(diagonal, 0, deep)

    def arrived(d):
        j = lax.rem(me + d, n)
        o_copy(j, j).wait_recv()
        l_copy(j, j).wait_recv()

    each(arrived)

    levels = lrecv[...]
    top = jnp.max(levels, axis=0)
    share = jnp.exp(levels - top[None])
    lrecv[...] = share / jnp.sum(share, axis=0)[None]
    accf[...] = jnp.zeros_like(accf)

    def merge(s, _):
        share_s = lrecv[s]
        for h in range(heads):
            accf[h] += share_s[:, h:h + 1] * orecv[s, h].astype(f32)
        return _

    lax.fori_loop(0, n + 1, merge, 0)
    for h in range(heads):
        attg[me, :, h * HD:(h + 1) * HD] = accf[h].astype(bf16)
    results.begin()
    results.forward(0)
    each(results.spread, 1, deep)
    each(results.forward, 1, deep)
    out_weight.wait()
    each(results.finish, 0, deep)

    half = rows // 2
    attended = attg[...].astype(f32).reshape(rows, qcols).astype(bf16)
    part = jnp.dot(attended, wo[...], preferred_element_type=f32)
    pf[...] = part.reshape(2, half, part.shape[1])
    msend[...] = pf[1 - core].astype(bf16)
    swap = pltpu.make_async_remote_copy(
        src_ref=msend, dst_ref=mrecv, send_sem=m_sem.at[0], recv_sem=m_sem.at[1],
        device_id={"mp": 1 - core}, device_id_type=pl.DeviceIdType.MESH)
    swap.start()

    def sent(d):
        x_copy(d).wait_send()
        j = lax.rem(me + d, n)
        o_copy(j, me).wait_send()
        l_copy(j, me).wait_send()

    each(sent)

    def summed(dz):
        for kind in (1, 2, 3):
            p_copy(dz, kind).wait_send()

    each(summed, 0, deep)
    each(lambda dz: z_copy(dz).wait_send(), 1, deep)
    queries.drain()
    results.drain()
    swap.wait()
    out_ref[...] = (pf[core] + mrecv[...].astype(f32)).astype(bf16)


def fused(n, layer_input, w_query, w_key, w_value, w_out, kv_cache, cache_len):
    rp = layer_input.shape[0]
    rows = rp * n
    depth = w_query.shape[0]
    steps = rows // cache_len.shape[0]
    heads = w_query.shape[1] // HD
    kvh = w_key.shape[1] // HD
    total = w_query.shape[1] + w_key.shape[1] + w_value.shape[1]
    per = rp // steps
    me = lax.axis_index("seq")
    lengths = lax.dynamic_slice_in_dim(cache_len, me * per, per, 0)
    positions = (lengths[:, None] + jnp.arange(steps, dtype=jnp.int32)[None, :]).reshape(rp)
    angles = positions.astype(jnp.float32)[:, None] * inverse_freq()
    cosine = jnp.cos(angles)
    sines = jnp.sin(angles)
    cosine = jnp.concatenate([cosine, cosine], axis=-1)
    sines = jnp.concatenate([-sines, sines], axis=-1)
    f32, bf16 = jnp.float32, jnp.bfloat16
    vm = pltpu.VMEM
    dma = pltpu.SemaphoreType.DMA
    vmem = pl.BlockSpec(memory_space=pltpu.VMEM)
    hbm = pl.BlockSpec(memory_space=pl.ANY)
    cols = w_out.shape[1]
    return pl.pallas_call(
        functools.partial(fused_kernel, n, steps, 1.0 / math.sqrt(HD)),
        out_shape=jax.ShapeDtypeStruct((rows // 2, cols), bf16),
        in_specs=[vmem, vmem, pl.BlockSpec(memory_space=pltpu.SMEM), vmem] + [hbm] * 5,
        out_specs=vmem,
        scratch_shapes=[
            vm(w_query.shape, bf16), vm(w_key.shape, bf16), vm(w_value.shape, bf16),
            vm(w_out.shape, bf16), vm(kv_cache.shape, bf16),
            vm((n, rp, depth), bf16), vm((n, rp, depth), bf16),
            vm((n, rp, total), bf16), vm((n // 4, 3, rp, total), bf16),
            vm((n // 4, rp, total), f32), vm((n // 4, rp, total), f32), vm((rp, total), f32),
            vm((n, heads, rp, HD), bf16), vm((kvh, HD, HD), bf16), vm((kvh, HD, HD), bf16),
            vm((n, heads, rp, HD), bf16), vm((n, rp, HD), f32),
            vm((n + 1, heads, rp, HD), bf16), vm((n + 1, rp, HD), f32),
            vm((heads, rp, HD), f32), vm((n, rp, heads * HD), bf16),
            vm((2, rows // 2, cols), f32), vm((rows // 2, cols), bf16), vm((rows // 2, cols), bf16),
            dma((4,)), dma((n,)),
        ] + [dma((n,))] * 6 + [dma((5, n // 4))] * 4 + [dma((n // 4, 4))] * 2 + [dma((n,))] * 2 + [dma((2,))],
        compiler_params=pltpu.CompilerParams(
            collective_id=0, has_side_effects=True, vmem_limit_bytes=56 * 1024 * 1024),
        name="decode_block",
    )(cosine, sines, cache_len, layer_input, w_query, w_key, w_value, w_out, kv_cache)


def block(n, mp, layer_input, w_query, w_key, w_value, w_out, kv_cache, cache_len):
    rp = layer_input.shape[0]
    steps = rp * n // cache_len.shape[0]
    heads = w_query.shape[1] // HD
    if mp == 2 and n == 16 and rp == 8 and rp % steps == 0 and heads <= HD:
        return fused(n, layer_input, w_query, w_key, w_value, w_out, kv_cache, cache_len)
    return shards(layer_input, w_query, w_key, w_value, w_out, kv_cache, cache_len)


def solution(mesh):
    return jax.shard_map(
        functools.partial(block, mesh.shape["seq"], mesh.shape["mp"]),
        mesh=mesh,
        in_specs=(
            P("seq", None),
            P("seq", "mp"),
            P("seq", "mp"),
            P("seq", "mp"),
            P("mp", "seq"),
            P(None, None, "seq", "mp"),
            P(),
        ),
        out_specs=P("mp", "seq"),
        check_vma=False,
    )
```

```python
import functools
import math

import jax
import jax.numpy as jnp
from jax import lax
from jax.experimental import pallas as pl
from jax.experimental.pallas import tpu as pltpu
from jax.sharding import PartitionSpec as P

HD = 128


NEG_FILL = -1e30


def inverse_freq():
    index = jnp.arange(HD // 2, dtype=jnp.float32)
    base_freq = jnp.exp(-(2.0 * index / HD) * math.log(500000.0))
    wavelength = 2.0 * math.pi / base_freq
    smooth = jnp.clip((8192.0 / wavelength - 1.0) / 3.0, 0.0, 1.0)
    return (1.0 - smooth) * base_freq / 8.0 + smooth * base_freq


def rotate(values, positions):
    angles = positions.astype(jnp.float32)[..., None] * inverse_freq()
    cosine = jnp.cos(angles)
    sines = jnp.sin(angles)
    half_width = HD // 2
    first_half = values[..., :half_width]
    second_half = values[..., half_width:]
    return jnp.concatenate(
        [first_half * cosine - second_half * sines, second_half * cosine + first_half * sines],
        axis=-1,
    )


def shards(layer_input, w_query, w_key, w_value, w_out, kv_cache, cache_len):
    widened = layer_input.astype(jnp.float32)
    normed = (
        widened * lax.rsqrt(jnp.mean(widened * widened, axis=-1, keepdims=True) + 1e-05)
    ).astype(jnp.bfloat16)
    gathered = lax.all_to_all(normed, "seq", split_axis=1, concat_axis=0, tiled=True)
    partial_query = jnp.dot(gathered, w_query, preferred_element_type=jnp.float32)
    partial_key = jnp.dot(gathered, w_key, preferred_element_type=jnp.float32)
    partial_value = jnp.dot(gathered, w_value, preferred_element_type=jnp.float32)
    row_count = gathered.shape[0]
    request_count = cache_len.shape[0]
    decode_count = row_count // request_count
    heads_here = partial_query.shape[1] // HD
    kv_here = partial_key.shape[1] // HD
    group_size = heads_here // kv_here
    score_scale = 1.0 / math.sqrt(HD)
    highest = lax.Precision.HIGHEST
    query_all, key_all, value_all = lax.psum((partial_query, partial_key, partial_value), "seq")
    positions = (cache_len[:, None] + jnp.arange(decode_count, dtype=jnp.int32)[None, :]).reshape(
        row_count
    )
    queries = rotate(query_all.reshape(row_count, heads_here, HD), positions[:, None]).astype(
        jnp.bfloat16
    )
    keys_new = rotate(key_all.reshape(row_count, kv_here, HD), positions[:, None]).astype(
        jnp.bfloat16
    )
    values_new = value_all.astype(jnp.bfloat16)
    queries = queries.reshape(request_count, decode_count, kv_here, group_size, HD)
    keys_new = keys_new.reshape(request_count, decode_count, kv_here, HD)
    values_new = values_new.reshape(request_count, decode_count, kv_here, HD)
    block_size = kv_cache.shape[2]
    cache_keys = kv_cache[0].reshape(request_count, block_size, kv_here, HD)
    cache_values = kv_cache[1].reshape(request_count, block_size, kv_here, HD).astype(jnp.float32)
    first_slot = lax.axis_index("seq") * block_size
    slot_index = first_slot + jnp.arange(block_size, dtype=jnp.int32)
    active_slot = (slot_index[None, :] < cache_len[:, None])[:, None, None, None, :]
    causal = (jnp.arange(decode_count)[:, None] >= jnp.arange(decode_count)[None, :])[
        None, None, None
    ]
    old_scores = (
        jnp.einsum("rtkgd,rpkd->rkgtp", queries, cache_keys, preferred_element_type=jnp.float32)
        * score_scale
    )
    old_scores = jnp.where(active_slot, old_scores, NEG_FILL)
    old_top = jnp.max(old_scores, axis=-1)
    new_scores = (
        jnp.einsum("rtkgd,rukd->rkgtu", queries, keys_new, preferred_element_type=jnp.float32)
        * score_scale
    )
    new_scores = jnp.where(causal, new_scores, NEG_FILL)
    new_top = jnp.max(new_scores, axis=-1)
    row_top = lax.pmax(jnp.maximum(old_top, new_top), "seq")
    old_weights = jnp.where(active_slot, jnp.exp(old_scores - row_top[..., None]), 0.0)
    old_total, old_pooled = lax.psum(
        (
            jnp.sum(old_weights, axis=-1),
            jnp.einsum("rkgtp,rpkd->rkgtd", old_weights, cache_values, precision=highest),
        ),
        "seq",
    )
    new_weights = jnp.where(causal, jnp.exp(new_scores - row_top[..., None]), 0.0)
    denominator = old_total + jnp.sum(new_weights, axis=-1)
    pooled = old_pooled + jnp.einsum(
        "rkgtu,rukd->rkgtd", new_weights, values_new.astype(jnp.float32), precision=highest
    )
    attended = (
        (pooled / denominator[..., None])
        .transpose(0, 3, 1, 2, 4)
        .reshape(row_count, heads_here * HD)
        .astype(jnp.bfloat16)
    )
    return lax.psum_scatter(
        jnp.dot(attended, w_out, preferred_element_type=jnp.float32).astype(jnp.bfloat16),
        "mp",
        scatter_dimension=0,
        tiled=True,
    )


def fused_kernel(
    n, steps, scale, cos_ref, sin_ref, len_ref, x_ref, wq_hbm, wk_hbm, wv_hbm, wo_hbm, kv_hbm,
    out_ref,
    wq, wk, wv, wo, kv, nsend, xrecv, psend, prec, zsend, zrecv, acc, qall, knew, vnew,
    osend, lsend, orecv, lrecv, accf, attg, pf, msend, mrecv,
    w_sem, kv_sem, s_x, r_x, s_o, r_o, s_l, r_l, s_q, r_q, s_a, r_a, s_p, r_p, s_z, r_z, m_sem,
):
    me = lax.axis_index("seq")
    core = lax.axis_index("mp")
    f32, bf16 = jnp.float32, jnp.bfloat16
    rp, width = x_ref.shape
    depth = width // n
    rows = n * rp
    heads = wq.shape[1] // HD
    kvh = wk.shape[1] // HD
    group = heads // kvh
    per = rp // steps
    block = kv.shape[2]
    qcols = heads * HD
    kcols = kvh * HD

    weights = [
        pltpu.make_async_copy(wq_hbm, wq, w_sem.at[0]),
        pltpu.make_async_copy(wk_hbm, wk, w_sem.at[1]),
        pltpu.make_async_copy(wv_hbm, wv, w_sem.at[2]),
    ]
    out_weight = pltpu.make_async_copy(wo_hbm, wo, w_sem.at[3])

    def cache_copy(j):
        at = (slice(None), pl.ds(j * per, per))
        return pltpu.make_async_copy(kv_hbm.at[at], kv.at[at], kv_sem.at[j])

    for copy in weights:
        copy.start()

    barrier = pltpu.get_barrier_semaphore()

    def greet(d, _):
        pl.semaphore_signal(barrier, inc=1, device_id={"seq": lax.rem(me + d, n)},
                            device_id_type=pl.DeviceIdType.MESH)
        return _

    lax.fori_loop(1, n, greet, 0)
    pl.semaphore_signal(barrier, inc=1, device_id={"mp": 1 - core},
                        device_id_type=pl.DeviceIdType.MESH)

    def remote(src, dst, send, recv, d):
        return pltpu.make_async_remote_copy(
            src_ref=src, dst_ref=dst, send_sem=send.at[d], recv_sem=recv.at[d],
            device_id={"seq": lax.rem(me + d, n)}, device_id_type=pl.DeviceIdType.MESH)

    def x_copy(d):
        return remote(nsend.at[lax.rem(me + d, n)], xrecv.at[me], s_x, r_x, d)

    def o_copy(j, slot):
        return pltpu.make_async_remote_copy(
            src_ref=osend.at[j], dst_ref=orecv.at[slot], send_sem=s_o.at[j], recv_sem=r_o.at[slot],
            device_id={"seq": j}, device_id_type=pl.DeviceIdType.MESH)

    def l_copy(j, slot):
        return pltpu.make_async_remote_copy(
            src_ref=lsend.at[j], dst_ref=lrecv.at[slot], send_sem=s_l.at[j], recv_sem=r_l.at[slot],
            device_id={"seq": j}, device_id_type=pl.DeviceIdType.MESH)

    deep = n // 4
    x_at, y_at, z_at = lax.rem(me, 2), lax.rem(lax.div(me, 2), 2), lax.div(me, 4)
    x_peer = me + 1 - 2 * x_at
    y_peer = me + 2 - 4 * y_at

    def source(kind, dz):
        z = lax.rem(z_at - dz + deep, deep)
        x = x_at + lax.rem(kind, 2) * (1 - 2 * x_at)
        y = y_at + lax.div(kind, 2) * (1 - 2 * y_at)
        return z * 4 + y * 2 + x

    def p_copy(dz, kind):
        return pltpu.make_async_remote_copy(
            src_ref=psend.at[source(kind, deep - dz)], dst_ref=prec.at[dz, kind - 1],
            send_sem=s_p.at[dz, kind], recv_sem=r_p.at[dz, kind],
            device_id={"seq": source(kind, 0)}, device_id_type=pl.DeviceIdType.MESH)

    def z_copy(dz):
        return remote(zsend.at[dz], zrecv.at[dz], s_z, r_z, 4 * dz)

    class Gather:
        def __init__(self, view, part, send, recv):
            self.whole = lambda j: view(j, 2 * part, 2 * part + 2)
            self.low = lambda j: view(j, 2 * part, 2 * part + 1)
            self.high = lambda j: view(j, 2 * part + 1, 2 * part + 2)
            self.part, self.send, self.recv = part, send, recv

        def copy(self, view, way, dz, target):
            return pltpu.make_async_remote_copy(
                src_ref=view, dst_ref=view, send_sem=self.send.at[self.part, way, dz],
                recv_sem=self.recv.at[self.part, way, dz],
                device_id={"seq": target}, device_id_type=pl.DeviceIdType.MESH)

        def z(self, dz):
            return self.copy(self.whole(me), 0, dz, lax.rem(me + 4 * dz, n))

        def x(self, dz):
            return self.copy(self.whole(source(0, dz)), 1, dz, x_peer)

        def y(self, dz):
            return self.copy(self.whole(source(0, dz)), 2, dz, y_peer)

        def xy(self, dz):
            return self.copy(self.low(source(1, dz)), 3, dz, y_peer)

        def yx(self, dz):
            return self.copy(self.high(source(2, dz)), 4, dz, x_peer)

        def begin(self):
            each(lambda dz: self.z(dz).start(), 1, deep)
            self.x(0).start()
            self.y(0).start()

        def spread(self, dz):
            self.z(dz).wait_recv()
            self.x(dz).start()
            self.y(dz).start()

        def forward(self, dz):
            self.x(dz).wait_recv()
            self.xy(dz).start()
            self.y(dz).wait_recv()
            self.yx(dz).start()

        def finish(self, dz):
            self.xy(dz).wait_recv()
            self.yx(dz).wait_recv()

        def sent(self, dz):
            self.x(dz).wait_send()
            self.y(dz).wait_send()
            self.xy(dz).wait_send()
            self.yx(dz).wait_send()

        def drain(self):
            each(lambda dz: self.z(dz).wait_send(), 1, deep)
            each(self.sent, 0, deep)

    def each(action, first=1, last=n):
        def body(d, _):
            action(d)
            return _
        lax.fori_loop(first, last, body, 0)

    hq, cq = heads // 4, qcols // 4
    queries = [Gather(lambda j, a, b: qall.at[j, a * hq:b * hq], part, s_q, r_q)
               for part in range(2)]
    results = [Gather(lambda j, a, b: attg.at[j, :, a * cq:b * cq], part, s_a, r_a)
               for part in range(2)]

    widened = x_ref[...].astype(f32)
    norm = widened * lax.rsqrt(jnp.mean(widened * widened, axis=-1, keepdims=True) + 1e-05)
    for j in range(n):
        nsend[j] = norm[:, j * depth:(j + 1) * depth].astype(bf16)
    xrecv[me] = nsend[me]
    pl.semaphore_wait(barrier, n)
    each(lambda d: x_copy(d).start())
    each(lambda d: cache_copy(d).start(), 0)
    out_weight.start()
    for copy in weights:
        copy.wait()
    each(lambda d: x_copy(d).wait_recv())

    gathered = xrecv[...].astype(f32).reshape(rows, depth).astype(bf16)

    def project(weight, count, first):
        tile = min(512, count)
        for c in range(count // tile):
            part = jnp.dot(gathered, weight[:, c * tile:(c + 1) * tile], preferred_element_type=f32)
            psend[:, :, first + c * tile:first + (c + 1) * tile] = part.reshape(
                n, rp, tile).astype(bf16)

    project(wq, qcols, 0)
    project(wk, kcols, qcols)
    project(wv, kcols, qcols + kcols)

    def release(dz):
        for kind in (3, 1, 2):
            p_copy(dz, kind).start()

    def plane_sum(dz):
        total = psend[source(0, deep - dz)].astype(f32)
        for kind in (3, 1, 2):
            p_copy(dz, kind).wait_recv()
        for kind in (3, 1, 2):
            total += prec[dz, kind - 1].astype(f32)
        return total

    def pass_on(dz):
        zsend[dz] = plane_sum(dz)
        z_copy(dz).start()

    def add(dz):
        z_copy(dz).wait_recv()
        acc[...] += zrecv[dz]

    each(release, 1, deep)
    release(0)
    each(pass_on, 1, deep)
    acc[...] = plane_sum(0)
    each(add, 1, deep)

    cosine = cos_ref[...]
    sines = sin_ref[...]

    def turn(column):
        value = acc[:, column:column + HD]
        return value * cosine + pltpu.roll(value, HD // 2, 1) * sines

    for part in range(2):
        for h in range(part * heads // 2, (part + 1) * heads // 2):
            qall[me, h] = turn(h * HD).astype(bf16)
        queries[part].begin()
    for k in range(kvh):
        knew[k] = jnp.zeros(knew.shape[1:], bf16)
        vnew[k] = jnp.zeros(vnew.shape[1:], bf16)
        knew[k, 0:rp] = turn(qcols + k * HD).astype(bf16)
        column = qcols + kcols + k * HD
        vnew[k, 0:rp] = acc[:, column:column + HD].astype(bf16)

    lane = lax.broadcasted_iota(jnp.int32, (rp, HD), 1)
    m_rows = group * rp

    def attend(query, keys, values, bias, o_ref, l_ref, at):
        stats = jnp.zeros((rp, HD), f32)
        for k in range(kvh):
            q = query(k).astype(f32).reshape(m_rows, HD).astype(bf16)
            scores = lax.dot_general(q, keys(k), (((1,), (1,)), ((), ())),
                                     preferred_element_type=f32) * scale + bias
            top = jnp.max(scores, axis=-1, keepdims=True)
            weight = jnp.exp(scores - top)
            total = jnp.sum(weight, axis=-1, keepdims=True)
            pooled = jnp.dot(weight.astype(bf16), values(k), preferred_element_type=f32)
            pooled = pooled * (1.0 / total)
            o_ref[at, k * group:(k + 1) * group] = pooled.reshape(group, rp, HD).astype(bf16)
            level = top + jnp.log(total)
            for g in range(group):
                stats = jnp.where(lane == k * group + g, level[g * rp:(g + 1) * rp], stats)
        l_ref[at] = stats

    new = knew.shape[1]
    row = lax.rem(lax.broadcasted_iota(jnp.int32, (m_rows, new), 0), rp)
    col = lax.broadcasted_iota(jnp.int32, (m_rows, new), 1)
    seen = (col <= row) & (lax.div(col, steps) == lax.div(row, steps))
    attend(lambda k: qall[me, k * group:(k + 1) * group], lambda k: knew[k], lambda k: vnew[k],
           jnp.where(seen, 0.0, NEG_FILL), orecv, lrecv, n)

    span = per * block
    row_request = lax.div(lax.rem(lax.broadcasted_iota(jnp.int32, (m_rows, span), 0), rp), steps)
    slot = lax.broadcasted_iota(jnp.int32, (m_rows, span), 1)

    def cached(j, o_ref, l_ref):
        cache_copy(j).wait()
        bias = jnp.full((m_rows, span), NEG_FILL, f32)
        for r in range(per):
            left = len_ref[j * per + r] - me * block
            live = (row_request == r) & (slot >= r * block) & (slot < r * block + jnp.minimum(left, block))
            bias = jnp.where(live, 0.0, bias)
        here = pl.ds(j * per, per)
        attend(lambda k: qall[j, k * group:(k + 1) * group],
               lambda k: kv[0, here, :, k * HD:(k + 1) * HD].reshape(span, HD),
               lambda k: kv[1, here, :, k * HD:(k + 1) * HD].reshape(span, HD),
               bias, o_ref, l_ref, j)

    def answer(j):
        cached(j, osend, lsend)
        o_copy(j, me).start()
        l_copy(j, me).start()

    queries[0].forward(0)
    queries[1].forward(0)
    cached(me, orecv, lrecv)
    each(queries[0].spread, 1, deep)
    each(queries[1].spread, 1, deep)

    def own_line(dz):
        answer(source(0, dz))
        queries[0].forward(dz)
        queries[1].forward(dz)

    each(own_line, 1, deep)
    each(lambda i: answer(source(1 + lax.div(i, deep), lax.rem(i, deep))), 0, 2 * deep)

    def diagonal(dz):
        queries[0].finish(dz)
        queries[1].finish(dz)
        answer(source(3, dz))

    each(diagonal, 0, deep)

    def arrived(d):
        j = lax.rem(me + d, n)
        o_copy(j, j).wait_recv()
        l_copy(j, j).wait_recv()

    each(arrived)

    levels = lrecv[...]
    top = jnp.max(levels, axis=0)
    share = jnp.exp(levels - top[None])
    lrecv[...] = share / jnp.sum(share, axis=0)[None]
    accf[...] = jnp.zeros_like(accf)

    for part in range(2):
        mine = range(part * heads // 2, (part + 1) * heads // 2)

        def merge(s, _):
            share_s = lrecv[s]
            for h in mine:
                accf[h] += share_s[:, h:h + 1] * orecv[s, h].astype(f32)
            return _

        lax.fori_loop(0, n + 1, merge, 0)
        for h in mine:
            attg[me, :, h * HD:(h + 1) * HD] = accf[h].astype(bf16)
        results[part].begin()
    for part in range(2):
        results[part].forward(0)
        each(results[part].spread, 1, deep)
    for part in range(2):
        each(results[part].forward, 1, deep)
    out_weight.wait()

    half = rows // 2
    part_cols = qcols // 2
    for part in range(2):
        each(results[part].finish, 0, deep)
        at = slice(part * part_cols, (part + 1) * part_cols)
        attended = attg[:, :, at].astype(f32).reshape(rows, part_cols).astype(bf16)
        product = jnp.dot(attended, wo[at], preferred_element_type=f32)
        product = product.reshape(2, half, product.shape[1])
        if part == 0:
            pf[...] = product
        else:
            pf[...] += product
    msend[...] = pf[1 - core].astype(bf16)
    swap = pltpu.make_async_remote_copy(
        src_ref=msend, dst_ref=mrecv, send_sem=m_sem.at[0], recv_sem=m_sem.at[1],
        device_id={"mp": 1 - core}, device_id_type=pl.DeviceIdType.MESH)
    swap.start()

    def sent(d):
        x_copy(d).wait_send()
        j = lax.rem(me + d, n)
        o_copy(j, me).wait_send()
        l_copy(j, me).wait_send()

    each(sent)

    def summed(dz):
        for kind in (1, 2, 3):
            p_copy(dz, kind).wait_send()

    each(summed, 0, deep)
    each(lambda dz: z_copy(dz).wait_send(), 1, deep)
    for gather in queries + results:
        gather.drain()
    swap.wait()
    out_ref[...] = (pf[core] + mrecv[...].astype(f32)).astype(bf16)


def fused(n, layer_input, w_query, w_key, w_value, w_out, kv_cache, cache_len):
    rp = layer_input.shape[0]
    rows = rp * n
    depth = w_query.shape[0]
    steps = rows // cache_len.shape[0]
    heads = w_query.shape[1] // HD
    kvh = w_key.shape[1] // HD
    total = w_query.shape[1] + w_key.shape[1] + w_value.shape[1]
    per = rp // steps
    me = lax.axis_index("seq")
    lengths = lax.dynamic_slice_in_dim(cache_len, me * per, per, 0)
    positions = (lengths[:, None] + jnp.arange(steps, dtype=jnp.int32)[None, :]).reshape(rp)
    angles = positions.astype(jnp.float32)[:, None] * inverse_freq()
    cosine = jnp.cos(angles)
    sines = jnp.sin(angles)
    cosine = jnp.concatenate([cosine, cosine], axis=-1)
    sines = jnp.concatenate([-sines, sines], axis=-1)
    f32, bf16 = jnp.float32, jnp.bfloat16
    vm = pltpu.VMEM
    dma = pltpu.SemaphoreType.DMA
    vmem = pl.BlockSpec(memory_space=pltpu.VMEM)
    hbm = pl.BlockSpec(memory_space=pl.ANY)
    cols = w_out.shape[1]
    return pl.pallas_call(
        functools.partial(fused_kernel, n, steps, 1.0 / math.sqrt(HD)),
        out_shape=jax.ShapeDtypeStruct((rows // 2, cols), bf16),
        in_specs=[vmem, vmem, pl.BlockSpec(memory_space=pltpu.SMEM), vmem] + [hbm] * 5,
        out_specs=vmem,
        scratch_shapes=[
            vm(w_query.shape, bf16), vm(w_key.shape, bf16), vm(w_value.shape, bf16),
            vm(w_out.shape, bf16), vm(kv_cache.shape, bf16),
            vm((n, rp, depth), bf16), vm((n, rp, depth), bf16),
            vm((n, rp, total), bf16), vm((n // 4, 3, rp, total), bf16),
            vm((n // 4, rp, total), f32), vm((n // 4, rp, total), f32), vm((rp, total), f32),
            vm((n, heads, rp, HD), bf16), vm((kvh, HD, HD), bf16), vm((kvh, HD, HD), bf16),
            vm((n, heads, rp, HD), bf16), vm((n, rp, HD), f32),
            vm((n + 1, heads, rp, HD), bf16), vm((n + 1, rp, HD), f32),
            vm((heads, rp, HD), f32), vm((n, rp, heads * HD), bf16),
            vm((2, rows // 2, cols), f32), vm((rows // 2, cols), bf16), vm((rows // 2, cols), bf16),
            dma((4,)), dma((n,)),
        ] + [dma((n,))] * 6 + [dma((2, 5, n // 4))] * 4 + [dma((n // 4, 4))] * 2 + [dma((n,))] * 2 + [dma((2,))],
        compiler_params=pltpu.CompilerParams(
            collective_id=0, has_side_effects=True, vmem_limit_bytes=56 * 1024 * 1024),
        name="decode_block",
    )(cosine, sines, cache_len, layer_input, w_query, w_key, w_value, w_out, kv_cache)


def block(n, mp, layer_input, w_query, w_key, w_value, w_out, kv_cache, cache_len):
    rp = layer_input.shape[0]
    steps = rp * n // cache_len.shape[0]
    heads = w_query.shape[1] // HD
    if mp == 2 and n == 16 and rp == 8 and rp % steps == 0 and heads <= HD and heads % 4 == 0:
        return fused(n, layer_input, w_query, w_key, w_value, w_out, kv_cache, cache_len)
    return shards(layer_input, w_query, w_key, w_value, w_out, kv_cache, cache_len)


def solution(mesh):
    return jax.shard_map(
        functools.partial(block, mesh.shape["seq"], mesh.shape["mp"]),
        mesh=mesh,
        in_specs=(
            P("seq", None),
            P("seq", "mp"),
            P("seq", "mp"),
            P("seq", "mp"),
            P("mp", "seq"),
            P(None, None, "seq", "mp"),
            P(),
        ),
        out_specs=P("mp", "seq"),
        check_vma=False,
    )
```
